32 devices in a mesh: grp: 16 (over z, y, core), sub: 2 (over x).
Axes of the slice: x: 2, y: 2, z: 4, core: 2. Of those that a mesh axis runs over, the one named last changes fastest.
Arguments:
- displacement: float32 [128, 32, 256], P('grp', 'sub'), may hold values from -2 to 2
- load: float32 [128, 32, 256], P('grp', 'sub'), may hold values from -6 to 6
- kl_coef: float32 [32], replicated, may hold values from -3 to 3
- damaged: int32 [16], replicated, may hold values from 0 to 1048575, as said below
- owner: int32 [16], replicated, may hold values from 0 to 15, each once
- phase: float32 [16, 32, 1024], P('grp', 'sub'), may hold values from 1 to 10
- soften: float32 [16, 32, 1024], P('grp', 'sub'), may hold values from 0.5 to 4
Outputs:
- step_field: float32 [128, 32, 256], P('grp', 'sub')
- residual: float32 [128, 32, 256], P('grp', 'sub')
- tangents: float32 [16, 9], replicated
- point_flux: float32 [16, 3], replicated
The draws below stay inside these ranges and needn't reach their ends.
Inputs may be any that keep to these rules, and one draw needn't show every extreme that they name: `damaged`: point p lies in rows p * 8 to (p + 1) * 8 - 1 of the first dimension, so the points are distinct cells. `owner`: each periodic cell resolves exactly one damaged point.
All inputs are finite; a program needn't handle non-finite values.
Results may differ from the reference program's by a relative error of at most 0.00045.
Values sent between devices are 32-bit elements; how exact they have to be, the bound alone decides.
A program may use at most 320 MiB of HBM per device.

```python
import math
import jax
import jax.numpy as jnp
from jax import lax

CX = 8
M = 32
MITERS = 4
CG_ITERS = 6
MODES = 32
NX = 128
NY = 32
NZ = 256
RVES = 16
DAMAGED = 16


def draw_damaged(key, part):
    key_x = jax.random.fold_in(key, 11)
    key_y = jax.random.fold_in(key, 12)
    key_z = jax.random.fold_in(key, 13)
    index = jnp.arange(DAMAGED, dtype=jnp.int32)
    rows_x = index * CX + jax.random.randint(key_x, (DAMAGED,), 0, CX, dtype=jnp.int32)
    rows_y = jax.random.randint(key_y, (DAMAGED,), 0, NY, dtype=jnp.int32)
    rows_z = jax.random.randint(key_z, (DAMAGED,), 0, NZ, dtype=jnp.int32)
    return ((rows_x * NY + rows_y) * NZ + rows_z).astype(jnp.int32)


def block_levels(own_key, dims, shards, low, largest):
    gain = 1.0
    for axis_at, blocks in shards:
        steps = jax.random.uniform(jax.random.fold_in(jax.random.fold_in(own_key, 6), axis_at), (blocks,), jnp.float32, low / len(shards), largest / len(shards))
        gain = gain * jnp.repeat(jnp.exp(steps), dims[axis_at] // blocks).reshape((-1,) + (1,) * (len(dims) - 1 - axis_at))
    return gain


def normal_values(own_key, shape, scale, reach, shards=(), kind=jnp.bfloat16):
    loudness = block_levels(own_key, shape, shards, -0.22, 0.18) if shards else 1.0
    result = jax.random.normal(own_key, shape, jnp.float32) * scale * loudness
    return jnp.minimum(jnp.maximum(result, -reach), reach).astype(kind)


def setup_inputs(seed: int = 0) -> dict:
    key_list = jax.random.split(jax.random.key(seed), 8)
    return {
        "displacement": normal_values(key_list[0], (NX, NY, NZ), 0.3, 2.0, ((0, 16), (1, 2)), jnp.float32),
        "load": normal_values(key_list[1], (NX, NY, NZ), 1.0, 6.0, ((0, 16), (1, 2)), jnp.float32),
        "kl_coef": normal_values(key_list[2], (MODES,), 1.0, 3.0, (), jnp.float32),
        "damaged": draw_damaged(jax.random.fold_in(key_list[7], 71), 0),
        "owner": jax.random.permutation(key_list[4], RVES).astype(jnp.int32),
        "phase": jnp.clip(jnp.exp(math.log(10.0) - 2.3025851 * jax.random.uniform(key_list[5], (RVES, M, M * M), jnp.float32) ** block_levels(key_list[5], (RVES, M, M * M), ((0, 16), (1, 2)), -0.2, 0.2)), 1.0, 10.0),
        "soften": jnp.clip(jnp.exp(math.log(4.0) - 2.0794415 * jax.random.uniform(key_list[6], (RVES, M, M * M), jnp.float32) ** block_levels(key_list[6], (RVES, M, M * M), ((0, 16), (1, 2)), -0.2, 0.2)), 0.5, 4.0),
    }


K0 = 6.0
SHIFT = 0.002
HIGH = lax.Precision.HIGHEST


def conductivity(kl_coef, xs, ys, zs, total_x, total_y, total_z):
    order = jnp.arange(4, dtype=jnp.float32)[:, None] + 1.0
    base_x = jnp.cos(jnp.pi * order * (xs.astype(jnp.float32)[None] + 0.5) / total_x)
    base_y = jnp.cos(jnp.pi * order * (ys.astype(jnp.float32)[None] + 0.5) / total_y)
    base_z = jnp.cos(jnp.pi * order[:2] * (zs.astype(jnp.float32)[None] + 0.5) / total_z)
    coef = kl_coef.reshape(2, 4, 4)
    field = jnp.einsum("cba,ai,bj,ck->ijk", coef, base_x, base_y, base_z, precision=HIGH)
    return jnp.exp(0.4 * field)


def gradient(field):
    padded = jnp.pad(field, ((0, 1), (0, 1), (0, 1)))
    return jnp.stack([padded[1:, :-1, :-1] - field, padded[:-1, 1:, :-1] - field, padded[:-1, :-1, 1:] - field])


def divergence(grads, field, kcell, damaged, tensors):
    flux = kcell[None] * grads
    picked = grads.reshape(3, -1)[:, damaged]
    newval = jnp.einsum("pij,jp->ip", tensors, picked, precision=HIGH)
    flux = flux.reshape(3, -1).at[:, damaged].set(newval).reshape(grads.shape)
    padded = jnp.pad(flux, ((0, 0), (1, 0), (1, 0), (1, 0)))
    out = padded[0, :-1, 1:, 1:] - flux[0] + padded[1, 1:, :-1, 1:] - flux[1] + padded[2, 1:, 1:, :-1] - flux[2]
    return out + SHIFT * field


def micro(args):
    phase, soften, strain = args
    cond = (phase / (1.0 + soften * jnp.sum(strain * strain))).reshape(M, M, M)
    freq = jnp.arange(M, dtype=jnp.int32)
    line = 4.0 * jnp.sin(jnp.pi * freq.astype(jnp.float32) / M) ** 2
    lam = line[:, None, None] + line[None, :, None] + line[None, None, :]
    anchor = ((freq[:, None, None] + freq[None, :, None] + freq[None, None, :]) == 0).astype(jnp.float32)
    inverse = (1.0 - anchor) / (K0 * (lam + anchor))
    units = jnp.eye(3, dtype=jnp.float32)

    def strains(phi):
        return [units[:, i][:, None, None, None] + jnp.roll(phi, -1, axis=i + 1) - phi for i in range(3)]

    phi = jnp.zeros((3, M, M, M), jnp.float32)
    for sweep in range(MITERS):
        parts = strains(phi)
        tau = [(cond - K0) * parts[i] for i in range(3)]
        div = tau[0] - jnp.roll(tau[0], 1, axis=1)
        div = div + tau[1] - jnp.roll(tau[1], 1, axis=2)
        div = div + tau[2] - jnp.roll(tau[2], 1, axis=3)
        spectrum = jnp.fft.fftn(div, axes=(1, 2, 3)) * inverse
        phi = jnp.real(jnp.fft.ifftn(spectrum, axes=(1, 2, 3)))
    parts = strains(phi)
    table = jnp.stack([jnp.mean(cond * parts[i], axis=(1, 2, 3)) for i in range(3)])
    return 0.5 * (table + table.T)


def reference(displacement, load, kl_coef, damaged, owner, phase, soften):
    nx, ny, nz = displacement.shape
    kcell = conductivity(kl_coef, jnp.arange(nx), jnp.arange(ny), jnp.arange(nz), nx, ny, nz)
    grads = gradient(displacement)
    strain = grads.reshape(3, -1)[:, damaged].T
    select = (owner[None, :] == jnp.arange(RVES, dtype=jnp.int32)[:, None]).astype(jnp.float32)
    rve_strain = jnp.sum(select[:, :, None] * strain[None], axis=1)
    tangents = lax.map(micro, (phase, soften, rve_strain))
    tensors = tangents[owner]

    def operate(field):
        return divergence(gradient(field), field, kcell, damaged, tensors)

    rhs = load - divergence(grads, displacement, kcell, damaged, tensors)
    step_field = jnp.zeros_like(rhs)
    residual = rhs
    direction = rhs
    norm_now = jnp.sum(residual * residual)
    for sweep in range(CG_ITERS):
        image = operate(direction)
        alpha = norm_now / jnp.sum(direction * image)
        step_field = step_field + alpha * direction
        residual = residual - alpha * image
        norm_next = jnp.sum(residual * residual)
        direction = residual + (norm_next / norm_now) * direction
        norm_now = norm_next
    step_grads = gradient(step_field).reshape(3, -1)[:, damaged].T
    point_flux = jnp.einsum("pij,pj->pi", tensors, step_grads, precision=HIGH)
    return step_field, residual, tangents.reshape(RVES, 9), point_flux
```

```python
import functools
import math

import jax
import jax.numpy as jnp
import numpy as np
from jax import lax
from jax.experimental import pallas as pl
from jax.experimental.pallas import tpu as pltpu
from jax.sharding import PartitionSpec as P

CG_ITERS = 6
STAGES = CG_ITERS + 1
K0 = 6.0
SHIFT = 0.002
MESH = pl.DeviceIdType.MESH
F32 = jnp.float32
BF16 = jnp.bfloat16


def split(x):
    high = x.astype(BF16)
    return high, (x - high.astype(F32)).astype(BF16)


def mm(a, b):
    return jnp.dot(a, b, preferred_element_type=F32)


def total(x):
    while x.ndim > 2:
        x = jnp.sum(x, axis=0)
    return jnp.sum(jnp.sum(x, axis=0, keepdims=True), axis=1, keepdims=True)


def kernel(
    n_grp, n_sub, side, coef, damaged, u_ref, load_ref, owner_ref, phase_ref, soften_ref, table_ref,
    inverse_ref, step_ref, res_ref, tan_ref, grad_ref, field, ys, hx, hy, hc, cells, bc,
    hsend, hrecv, csend, crecv, bsend, brecv, tsend, trecv,
):
    g = lax.axis_index("grp")
    s = lax.axis_index("sub")
    count = n_grp * n_sub
    me = g * n_sub + s
    rows_x, rows_y, rows_z = u_ref.shape
    planes = phase_ref.shape[0]
    total_x, total_y = rows_x * n_grp, rows_y * n_sub

    barrier = pltpu.get_barrier_semaphore()

    def greet(k, carry):
        other = lax.rem(me + k, count)
        pl.semaphore_signal(
            barrier, inc=1, device_id={"grp": other // n_sub, "sub": lax.rem(other, n_sub)},
            device_id_type=MESH,
        )
        return carry

    lax.fori_loop(1, count, greet, 0)
    pl.semaphore_wait(barrier, count - 1)

    g_up, g_down = lax.rem(g + 1, n_grp), lax.rem(g + n_grp - 1, n_grp)
    s_up, s_down = lax.rem(s + 1, n_sub), lax.rem(s + n_sub - 1, n_sub)

    def halo_start(stage, src):
        ys[stage, 0] = src[:, 0:1, :]
        ys[stage, 1] = src[:, rows_y - 1 : rows_y, :]
        moves = (
            (src.at[rows_x - 1], hx.at[stage, 0], g_up, s),
            (src.at[0], hx.at[stage, 1], g_down, s),
            (ys.at[stage, 1], hy.at[stage, 0], g, s_up),
            (ys.at[stage, 0], hy.at[stage, 1], g, s_down),
            (ys.at[stage, 0, rows_x - 1], hc.at[stage, 0], g_up, s_down),
            (ys.at[stage, 1, 0], hc.at[stage, 1], g_down, s_up),
        )
        copies = []
        for i, (a, b, to_g, to_s) in enumerate(moves):
            copy = pltpu.make_async_remote_copy(
                src_ref=a, dst_ref=b, send_sem=hsend.at[stage, i], recv_sem=hrecv.at[stage, i],
                device_id={"grp": to_g, "sub": to_s}, device_id_type=MESH,
            )
            copy.start()
            copies.append(copy)
        return copies

    def halo_wait(stage, copies):
        for copy in copies:
            copy.wait()
        low_x, high_x = (g > 0).astype(F32), (g < n_grp - 1).astype(F32)
        low_y, high_y = (s > 0).astype(F32), (s < n_sub - 1).astype(F32)
        return (
            hx[stage, 0] * low_x, hx[stage, 1] * high_x,
            hy[stage, 0] * low_y, hy[stage, 1] * high_y,
            hc[stage, 0] * (low_x * high_y), hc[stage, 1] * (high_x * low_y),
        )

    def spread_start(stage, row):
        bc[stage, me] = row

        def send(k, carry):
            other = lax.rem(me + k, count)
            pltpu.make_async_remote_copy(
                src_ref=bc.at[stage, me], dst_ref=bc.at[stage, me],
                send_sem=bsend.at[stage], recv_sem=brecv.at[stage],
                device_id={"grp": other // n_sub, "sub": lax.rem(other, n_sub)}, device_id_type=MESH,
            ).start()
            return carry

        lax.fori_loop(1, count, send, 0)

    def spread_wait(stage):
        most = bc.at[stage, pl.ds(0, count - 1)]
        pltpu.make_async_copy(most, most, brecv.at[stage]).wait()
        pltpu.make_async_copy(most, most, bsend.at[stage]).wait()
        return bc[stage]

    own = pl.ds(s * planes, planes)

    def cell_send(k, carry):
        to_s = lax.rem(s + k, n_sub)
        for i, ref in enumerate((phase_ref, soften_ref)):
            pltpu.make_async_remote_copy(
                src_ref=ref, dst_ref=cells.at[i, own], send_sem=csend.at[i], recv_sem=crecv.at[i],
                device_id={"grp": g, "sub": to_s}, device_id_type=MESH,
            ).start()
        return carry

    halo_u = halo_start(0, u_ref)
    lax.fori_loop(1, n_sub, cell_send, 0)
    cells[0, own] = phase_ref[...]
    cells[1, own] = soften_ref[...]

    block = (rows_x, rows_y, rows_z)
    at_x = lax.broadcasted_iota(jnp.int32, block, 0)
    at_y = lax.broadcasted_iota(jnp.int32, block, 1)
    at_z = lax.broadcasted_iota(jnp.int32, block, 2)
    lane = lax.broadcasted_iota(jnp.int32, (1, 128), 1)

    line_z = lax.broadcasted_iota(jnp.int32, (1, rows_z), 1).astype(F32) + 0.5
    cos_z = [jnp.cos(jnp.pi * (c + 1.0) * line_z / rows_z) for c in range(2)]
    pos_y = (s * rows_y + lax.broadcasted_iota(jnp.int32, (rows_y, rows_z), 0)).astype(F32) + 0.5
    low_y = (s * rows_y - 1 + lax.broadcasted_iota(jnp.int32, (1, rows_z), 0)).astype(F32) + 0.5
    pos_x = (g * rows_x + lax.broadcasted_iota(jnp.int32, (rows_x, 1, rows_z), 0)).astype(F32) + 0.5
    low_x = (g * rows_x - 1 + lax.broadcasted_iota(jnp.int32, (1, rows_z), 0)).astype(F32) + 0.5
    cos_y = [jnp.cos(jnp.pi * (b + 1.0) * pos_y / total_y) for b in range(4)]
    cos_yl = [jnp.cos(jnp.pi * (b + 1.0) * low_y / total_y) for b in range(4)]
    log_k = log_x = log_y = 0.0
    for a in range(4):
        rows = [
            coef[a + 4 * b] * cos_z[0] + coef[a + 4 * b + 16] * cos_z[1] for b in range(4)
        ]
        sheet = sum(rows[b] * cos_y[b] for b in range(4))
        strip = sum(rows[b] * cos_yl[b] for b in range(4))
        wave = jnp.cos(jnp.pi * (a + 1.0) * pos_x / total_x)
        log_k = log_k + wave * sheet[None]
        log_y = log_y + wave * strip[None]
        log_x = log_x + jnp.cos(jnp.pi * (a + 1.0) * low_x / total_x) * sheet
    k_own = jnp.exp(0.4 * log_k)
    k_x = jnp.exp(0.4 * log_x) * (g > 0).astype(F32)
    k_y = jnp.exp(0.4 * log_y) * (s > 0).astype(F32)

    def point(p):
        cell = damaged[p]
        rest = cell // rows_z
        return (
            rest // total_y - g * rows_x, lax.rem(rest, total_y) - s * rows_y, lax.rem(cell, rows_z)
        )

    px, py, pz = point(g)
    bx, by, bz = point(lax.max(g - 1, 0))
    hit = (at_x == px) & (at_y == py) & (at_z == pz)
    mask = jnp.where(hit, 1.0, 0.0)
    hit_x = (bx == -1) & (at_y[0] == by) & (at_z[0] == bz)
    mask_x = jnp.where(hit_x, 1.0, 0.0)
    hit_y = (py == -1) & (at_x[:, 0:1] == px) & (at_z[:, 0:1] == pz)
    mask_y = jnp.where(hit_y, 1.0, 0.0)

    def grads_of(v, halos):
        _, high_x, _, high_y, _, _ = halos
        dx = jnp.concatenate([v[1:], high_x[None]], 0) - v
        dy = jnp.where(at_y == rows_y - 1, high_y, pltpu.roll(v, rows_y - 1, 1)) - v
        dz = jnp.where(at_z == rows_z - 1, 0.0, pltpu.roll(v, rows_z - 1, 2)) - v
        return dx, dy, dz

    u = u_ref[...]
    halos_u = halo_wait(0, halo_u)
    grads_u = grads_of(u, halos_u)
    norm = sum(total(d * mask) ** 2 for d in grads_u)
    spread_start(0, jnp.where(lane == g, norm, 0.0))

    for i in range(2):
        most = cells.at[i, pl.ds(0, planes * (n_sub - 1))]
        pltpu.make_async_copy(most, most, crecv.at[i]).wait()
        pltpu.make_async_copy(most, most, csend.at[i]).wait()
    norms = jnp.sum(spread_wait(0), axis=0)
    strength = jnp.sum(jnp.where(owner_ref[...] == g, norms, 0.0), axis=1, keepdims=True)
    cond = cells[0] / (1.0 + cells[1] * strength)
    shift_k = cond - K0
    cube = (side, side, 128)
    cell_lane = lax.broadcasted_iota(jnp.int32, cube, 2)
    group = cell_lane // side
    in_group = lax.rem(cell_lane, side)

    def ahead(v, axis):
        if axis == 0:
            return jnp.concatenate([v[1:], v[:1]], 0)
        if axis == 1:
            return pltpu.roll(v, side - 1, 1)
        return jnp.where(in_group == side - 1, pltpu.roll(v, side - 1, 2), pltpu.roll(v, 127, 2))

    def behind(v, axis):
        if axis == 0:
            return jnp.concatenate([v[-1:], v[:-1]], 0)
        if axis == 1:
            return pltpu.roll(v, 1, 1)
        return jnp.where(in_group == 0, pltpu.roll(v, 129 - side, 2), pltpu.roll(v, 1, 2))

    wide = side * 8
    tz = table_ref[4, 0:128, 0:128], table_ref[5, 0:128, 0:128]
    ty = table_ref[0], table_ref[1]
    tx = table_ref[2], table_ref[3]

    def right(v):
        high, low = split(v.reshape(side * side, 128))
        return (mm(high, tz[0]) + mm(low, tz[0]) + mm(high, tz[1])).reshape(cube)

    def left(t, v):
        high, low = split(v)
        return mm(t[0], high) + mm(t[0], low) + mm(t[1], high)

    def along_y(v):
        flat = v.reshape(side * side, 128)
        parts = [left(ty, flat[i : i + wide]) for i in range(0, side * side, wide)]
        return jnp.concatenate(parts, 0).reshape(cube)

    def along_x(v):
        parts = [
            left(tx, v[:, i : i + 8].reshape(wide, 128)).reshape(side, 8, 128)
            for i in range(0, side, 8)
        ]
        return jnp.concatenate(parts, 1)

    def solve(div):
        spectrum = along_x(along_y(right(div))) * inverse_ref[...]
        return right(along_y(along_x(spectrum)))

    def div_of(phi):
        out = 0.0
        for axis in range(3):
            tau = shift_k * (ahead(phi, axis) - phi)
            out = out + tau - behind(tau, axis)
        return out

    back = jnp.where(group == 0, behind(shift_k, 0), shift_k)
    back = jnp.where(group == 1, behind(shift_k, 1), back)
    back = jnp.where(group == 2, behind(shift_k, 2), back)
    div1 = shift_k - back
    phi1 = solve(div1)
    div2 = div_of(phi1)
    phi2 = solve(div2)
    div3 = div_of(phi2)
    first, second = div1 + div2, div2 + div3
    points = float(side**3)
    mean = total(cond) / (points * (128 // side))
    entry = {}
    for turn in range(3):
        a = phi1 if turn == 0 else pltpu.roll(phi1, turn * side, 2)
        b = phi2 if turn == 0 else pltpu.roll(phi2, turn * side, 2)
        sums = jnp.sum(jnp.sum(a * first + b * second, axis=0), axis=0, keepdims=True)
        for j in range(turn, 3):
            value = -jnp.sum(
                jnp.where(lane // side == j, sums, 0.0), axis=1, keepdims=True
            ) / points
            entry[j - turn, j] = entry[j, j - turn] = value + mean if turn == 0 else value
    row = jnp.zeros((1, 128), F32)
    for i in range(3):
        for j in range(3):
            row = row + jnp.where(lane == 3 * i + j, entry[i, j], 0.0)
    tan_ref[g] = row

    def tangent_send(k, carry):
        pltpu.make_async_remote_copy(
            src_ref=tan_ref.at[g], dst_ref=tan_ref.at[g], send_sem=tsend, recv_sem=trecv,
            device_id={"grp": lax.rem(g + k, n_grp), "sub": s}, device_id_type=MESH,
        ).start()
        return carry

    lax.fori_loop(1, n_grp, tangent_send, 0)
    most = tan_ref.at[pl.ds(0, n_grp - 1)]
    pltpu.make_async_copy(most, most, trecv).wait()
    pltpu.make_async_copy(most, most, tsend).wait()
    tangents = tan_ref[...]
    which = lax.broadcasted_iota(jnp.int32, (n_grp, 1, 128), 0)

    def tensor(p):
        who = jnp.sum(jnp.where(lane == p, owner_ref[...], 0).astype(F32), axis=1, keepdims=True)
        mine = jnp.sum(jnp.where(which.astype(F32) == who, tangents, 0.0), axis=0)
        return {
            (i, j): jnp.sum(jnp.where(lane == 3 * i + j, mine, 0.0), axis=1, keepdims=True)
            for i in range(3) for j in range(i, 3)
        }

    t_own, t_before = tensor(g), tensor(lax.max(g - 1, 0))
    k00, k11, k22 = (k_own + mask * (t_own[i, i] - k_own) for i in range(3))
    k01, k02, k12 = (mask * t_own[i] for i in ((0, 1), (0, 2), (1, 2)))
    x00 = k_x + mask_x * (t_before[0, 0] - k_x)
    x01, x02 = mask_x * t_before[0, 1], mask_x * t_before[0, 2]
    y11 = k_y + mask_y * (t_own[1, 1] - k_y)
    y01, y12 = mask_y * t_own[0, 1], mask_y * t_own[1, 2]

    def operate(v, halos, grads):
        low_x, _, low_y, _, corner_x, corner_y = halos
        dx, dy, dz = grads
        q0 = k00 * dx + k01 * dy + k02 * dz
        q1 = k01 * dx + k11 * dy + k12 * dz
        q2 = k02 * dx + k12 * dy + k22 * dz
        edge_y, edge_z = at_y[0] == rows_y - 1, at_z[0] == rows_z - 1
        below_x = (
            x00 * (v[0] - low_x)
            + x01 * (jnp.where(edge_y, corner_x, pltpu.roll(low_x, rows_y - 1, 0)) - low_x)
            + x02 * (jnp.where(edge_z, 0.0, pltpu.roll(low_x, rows_z - 1, 1)) - low_x)
        )
        below_y = (
            y11 * (v[:, 0:1] - low_y)
            + y01 * (jnp.concatenate([low_y[1:], corner_y[None]], 0) - low_y)
            + y12
            * (jnp.where(at_z[:, 0:1] == rows_z - 1, 0.0, pltpu.roll(low_y, rows_z - 1, 2)) - low_y)
        )
        out = jnp.concatenate([below_x[None], q0[:-1]], 0) - q0
        out = out + jnp.where(at_y == 0, below_y, pltpu.roll(q1, 1, 1)) - q1
        out = out + jnp.where(at_z == 0, 0.0, pltpu.roll(q2, 1, 2)) - q2
        return out + SHIFT * v

    def picks(grads):
        return [total(d * mask) for d in grads]

    def row_of(values):
        out = jnp.zeros((1, 128), F32)
        for i, value in enumerate(values):
            out = out + jnp.where(lane == i, value, 0.0)
        return out

    r = load_ref[...] - operate(u, halos_u, grads_u)
    field[0] = r
    copies = halo_start(1, field.at[0])
    halos = halo_wait(1, copies)
    grads = grads_of(r, halos)
    w = operate(r, halos, grads)
    at_points = picks(grads)
    alpha = beta = gamma = None
    for step in range(CG_ITERS):
        last = step == CG_ITERS - 1
        if not last:
            field[step + 1] = w
            copies = halo_start(step + 2, field.at[step + 1])
        spread_start(step + 1, row_of([total(r * r), total(r * w)] + at_points))
        if not last:
            halos = halo_wait(step + 2, copies)
            grads = grads_of(w, halos)
            n = operate(w, halos, grads)
            at_points = picks(grads)
        got = spread_wait(step + 1)
        sums = jnp.sum(got, axis=0)
        new = sums[:, 0:1]
        delta = sums[:, 1:2]
        if step == 0:
            alpha = new / delta
            point_r = got
            point_p = point_r
            point_x = alpha * point_p
            p, sv = r, w
            x = alpha * p
        else:
            beta = new / gamma
            point_s = got if step == 1 else got + beta_before * point_s
            point_r = point_r - alpha * point_s
            alpha_new = new / (delta - beta * new / alpha)
            point_p = point_r + beta * point_p
            point_x = point_x + alpha_new * point_p
            alpha = alpha_new
            p = r + beta * p
            sv = w + beta * sv
            x = x + alpha * p
        r = r - alpha * sv
        if not last:
            z = n if step == 0 else n + beta * z
            w = w - alpha * z
        gamma, beta_before = new, beta
    step_ref[...] = x
    res_ref[...] = r
    grad_ref[...] = point_x


def tables(side):
    index = np.arange(side)
    angle = 2.0 * np.pi * (np.outer(index, index) % side) / side
    hartley = (np.cos(angle) + np.sin(angle)) / np.sqrt(side)
    wide = side * 8
    kinds = np.zeros((3, wide, wide), np.float64)
    kinds[0] = np.kron(np.eye(8), hartley)
    kinds[1] = np.kron(hartley, np.eye(8))
    kinds[2, :128, :128] = np.kron(np.eye(128 // side), hartley)
    kinds = kinds.astype(np.float32)
    high = kinds.astype(jnp.bfloat16)
    low = (kinds - high.astype(np.float32)).astype(jnp.bfloat16)
    table = np.stack([high, low], 1).reshape(6, wide, wide)
    line = 4.0 * np.sin(np.pi * index / side) ** 2
    lam = line[:, None, None] + line[None, :, None] + line[None, None, :]
    lam[0, 0, 0] = 1.0
    inverse = 1.0 / (K0 * lam)
    inverse[0, 0, 0] = 0.0
    return table, np.tile(inverse.astype(np.float32), (1, 1, 128 // side))


def body(displacement, load, kl_coef, damaged, owner, phase, soften):
    n_grp, n_sub = lax.axis_size("grp"), lax.axis_size("sub")
    count = n_grp * n_sub
    rows_x, rows_y, rows_z = displacement.shape
    planes = phase.shape[1]
    side = math.isqrt(phase.shape[2])
    table, inverse = tables(side)
    lanes = [
        jnp.tile(a.reshape(planes, side, side), (1, 1, 128 // side)) for a in (phase, soften)
    ]
    points = owner.shape[0]
    owners = jnp.pad(owner, (0, 128 - points), constant_values=-1).reshape(1, 128)
    vmem = pl.BlockSpec(memory_space=pltpu.VMEM)
    smem = pl.BlockSpec(memory_space=pltpu.SMEM)
    step_field, residual, rows, slopes = pl.pallas_call(
        functools.partial(kernel, n_grp, n_sub, side),
        out_shape=[
            jax.ShapeDtypeStruct(displacement.shape, F32),
            jax.ShapeDtypeStruct(displacement.shape, F32),
            jax.ShapeDtypeStruct((n_grp, 1, 128), F32),
            jax.ShapeDtypeStruct((count, 1, 128), F32),
        ],
        in_specs=[smem, smem] + [vmem] * 7,
        out_specs=[vmem] * 4,
        scratch_shapes=[
            pltpu.VMEM((CG_ITERS, rows_x, rows_y, rows_z), F32),
            pltpu.VMEM((STAGES, 2, rows_x, 1, rows_z), F32),
            pltpu.VMEM((STAGES, 2, rows_y, rows_z), F32),
            pltpu.VMEM((STAGES, 2, rows_x, 1, rows_z), F32),
            pltpu.VMEM((STAGES, 2, 1, rows_z), F32),
            pltpu.VMEM((2, side, side, 128), F32),
            pltpu.VMEM((STAGES, count, 1, 128), F32),
            pltpu.SemaphoreType.DMA((STAGES, 6)),
            pltpu.SemaphoreType.DMA((STAGES, 6)),
            pltpu.SemaphoreType.DMA((2,)),
            pltpu.SemaphoreType.DMA((2,)),
            pltpu.SemaphoreType.DMA((STAGES,)),
            pltpu.SemaphoreType.DMA((STAGES,)),
            pltpu.SemaphoreType.DMA,
            pltpu.SemaphoreType.DMA,
        ],
        compiler_params=pltpu.CompilerParams(collective_id=0, has_side_effects=True),
    )(kl_coef, damaged, displacement, load, owners, *lanes, jnp.asarray(table), jnp.asarray(inverse))
    tangents = rows[:, 0, :9]
    slopes = jnp.sum(slopes.reshape(points, -1, 128), axis=1)[:, 2:5]
    tensors = tangents[owner].reshape(-1, 3, 3)
    point_flux = jnp.sum(tensors * slopes[:, None, :], axis=2)
    return step_field, residual, tangents, point_flux


def solution(mesh):
    return jax.shard_map(
        body,
        mesh=mesh,
        in_specs=(
            P("grp", "sub", None), P("grp", "sub", None), P(), P(), P(),
            P("grp", "sub", None), P("grp", "sub", None),
        ),
        out_specs=(P("grp", "sub", None), P("grp", "sub", None), P(), P()),
        check_vma=False,
    )
```

```python
import functools
import math

import jax
import jax.numpy as jnp
import numpy as np
from jax import lax
from jax.experimental import pallas as pl
from jax.experimental.pallas import tpu as pltpu
from jax.sharding import PartitionSpec as P

CG_ITERS = 6
STAGES = CG_ITERS + 1
K0 = 6.0
SHIFT = 0.002
MESH = pl.DeviceIdType.MESH
F32 = jnp.float32
BF16 = jnp.bfloat16


def split(x):
    high = x.astype(BF16)
    return high, (x - high.astype(F32)).astype(BF16)


def mm(a, b):
    return jnp.dot(a, b, preferred_element_type=F32)


def total(x):
    while x.ndim > 2:
        x = jnp.sum(x, axis=0)
    return jnp.sum(jnp.sum(x, axis=0, keepdims=True), axis=1, keepdims=True)


def kernel(
    n_grp, n_sub, side, coef, damaged, owners, u_ref, load_ref, owner_ref, cell_ref, table_any,
    inverse_any, step_ref, res_ref, tan_ref, flux_ref, field, ys, hx, hy, hc, cells, bc, chosen,
    table_ref, inverse_ref, hsend, hrecv, csend, crecv, bsend, brecv, tsend, trecv, fetch,
):
    g = lax.axis_index("grp")
    s = lax.axis_index("sub")
    count = n_grp * n_sub
    me = g * n_sub + s
    rows_x, rows_y, rows_z = u_ref.shape
    planes = cell_ref.shape[0]
    total_x, total_y = rows_x * n_grp, rows_y * n_sub

    fetches = [
        pltpu.make_async_copy(a, b, fetch.at[i])
        for i, (a, b) in enumerate(((table_any, table_ref), (inverse_any, inverse_ref)))
    ]
    for copy in fetches:
        copy.start()
    barrier = pltpu.get_barrier_semaphore()

    def greet(k, carry):
        other = lax.rem(me + k, count)
        pl.semaphore_signal(
            barrier, inc=1, device_id={"grp": other // n_sub, "sub": lax.rem(other, n_sub)},
            device_id_type=MESH,
        )
        return carry

    lax.fori_loop(1, count, greet, 0)
    block = (rows_x, rows_y, rows_z)
    at_x = lax.broadcasted_iota(jnp.int32, block, 0)
    at_y = lax.broadcasted_iota(jnp.int32, block, 1)
    at_z = lax.broadcasted_iota(jnp.int32, block, 2)
    lane = lax.broadcasted_iota(jnp.int32, (1, 128), 1)

    line_z = lax.broadcasted_iota(jnp.int32, (1, rows_z), 1).astype(F32) + 0.5
    cos_z = [jnp.cos(jnp.pi * (c + 1.0) * line_z / rows_z) for c in range(2)]
    pos_y = (s * rows_y + lax.broadcasted_iota(jnp.int32, (rows_y, rows_z), 0)).astype(F32) + 0.5
    low_y = (s * rows_y - 1 + lax.broadcasted_iota(jnp.int32, (1, rows_z), 0)).astype(F32) + 0.5
    pos_x = (g * rows_x + lax.broadcasted_iota(jnp.int32, (rows_x, 1, rows_z), 0)).astype(F32) + 0.5
    low_x = (g * rows_x - 1 + lax.broadcasted_iota(jnp.int32, (1, rows_z), 0)).astype(F32) + 0.5
    cos_y = [jnp.cos(jnp.pi * (b + 1.0) * pos_y / total_y) for b in range(4)]
    cos_yl = [jnp.cos(jnp.pi * (b + 1.0) * low_y / total_y) for b in range(4)]
    log_k = log_x = log_y = 0.0
    for a in range(4):
        rows = [
            coef[a + 4 * b] * cos_z[0] + coef[a + 4 * b + 16] * cos_z[1] for b in range(4)
        ]
        sheet = sum(rows[b] * cos_y[b] for b in range(4))
        strip = sum(rows[b] * cos_yl[b] for b in range(4))
        wave = jnp.cos(jnp.pi * (a + 1.0) * pos_x / total_x)
        log_k = log_k + wave * sheet[None]
        log_y = log_y + wave * strip[None]
        log_x = log_x + jnp.cos(jnp.pi * (a + 1.0) * low_x / total_x) * sheet
    k_own = jnp.exp(0.4 * log_k)
    k_x = jnp.exp(0.4 * log_x) * (g > 0).astype(F32)
    k_y = jnp.exp(0.4 * log_y) * (s > 0).astype(F32)

    def point(p):
        cell = damaged[p]
        rest = cell // rows_z
        return (
            rest // total_y - g * rows_x, lax.rem(rest, total_y) - s * rows_y, lax.rem(cell, rows_z)
        )

    px, py, pz = point(g)
    bx, by, bz = point(lax.max(g - 1, 0))
    hit = (at_x == px) & (at_y == py) & (at_z == pz)
    mask = jnp.where(hit, 1.0, 0.0)
    hit_x = (bx == -1) & (at_y[0] == by) & (at_z[0] == bz)
    mask_x = jnp.where(hit_x, 1.0, 0.0)
    hit_y = (py == -1) & (at_x[:, 0:1] == px) & (at_z[:, 0:1] == pz)
    mask_y = jnp.where(hit_y, 1.0, 0.0)

    pl.semaphore_wait(barrier, count - 1)

    g_up, g_down = lax.rem(g + 1, n_grp), lax.rem(g + n_grp - 1, n_grp)
    s_up, s_down = lax.rem(s + 1, n_sub), lax.rem(s + n_sub - 1, n_sub)

    def halo_start(stage, src):
        ys[stage, 0] = src[:, 0:1, :]
        ys[stage, 1] = src[:, rows_y - 1 : rows_y, :]
        moves = (
            (src.at[rows_x - 1], hx.at[stage, 0], g_up, s),
            (src.at[0], hx.at[stage, 1], g_down, s),
            (ys.at[stage, 1], hy.at[stage, 0], g, s_up),
            (ys.at[stage, 0], hy.at[stage, 1], g, s_down),
            (ys.at[stage, 0, rows_x - 1], hc.at[stage, 0], g_up, s_down),
            (ys.at[stage, 1, 0], hc.at[stage, 1], g_down, s_up),
        )
        copies = []
        for i, (a, b, to_g, to_s) in enumerate(moves):
            copy = pltpu.make_async_remote_copy(
                src_ref=a, dst_ref=b, send_sem=hsend.at[stage, i], recv_sem=hrecv.at[stage, i],
                device_id={"grp": to_g, "sub": to_s}, device_id_type=MESH,
            )
            copy.start()
            copies.append(copy)
        return copies

    def halo_wait(stage, copies):
        for copy in copies:
            copy.wait()
        low_x, high_x = (g > 0).astype(F32), (g < n_grp - 1).astype(F32)
        low_y, high_y = (s > 0).astype(F32), (s < n_sub - 1).astype(F32)
        return (
            hx[stage, 0] * low_x, hx[stage, 1] * high_x,
            hy[stage, 0] * low_y, hy[stage, 1] * high_y,
            hc[stage, 0] * (low_x * high_y), hc[stage, 1] * (high_x * low_y),
        )

    def spread_start(stage, row):
        bc[stage, me] = row

        def send(k, carry):
            other = lax.rem(me + k, count)
            pltpu.make_async_remote_copy(
                src_ref=bc.at[stage, me], dst_ref=bc.at[stage, me],
                send_sem=bsend.at[stage], recv_sem=brecv.at[stage],
                device_id={"grp": other // n_sub, "sub": lax.rem(other, n_sub)}, device_id_type=MESH,
            ).start()
            return carry

        lax.fori_loop(1, count, send, 0)

    def spread_wait(stage):
        most = bc.at[stage, pl.ds(0, count - 1)]
        pltpu.make_async_copy(most, most, brecv.at[stage]).wait()
        pltpu.make_async_copy(most, most, bsend.at[stage]).wait()
        return bc[stage]

    own = pl.ds(s * planes, planes)

    def cell_send(k, carry):
        to_s = lax.rem(s + k, n_sub)
        pltpu.make_async_remote_copy(
            src_ref=cell_ref, dst_ref=cells.at[own], send_sem=csend, recv_sem=crecv,
            device_id={"grp": g, "sub": to_s}, device_id_type=MESH,
        ).start()
        return carry

    halo_u = halo_start(0, u_ref)
    lax.fori_loop(1, n_sub, cell_send, 0)
    cells[own] = cell_ref[...]

    def grads_of(v, halos):
        _, high_x, _, high_y, _, _ = halos
        dx = jnp.concatenate([v[1:], high_x[None]], 0) - v
        dy = jnp.where(at_y == rows_y - 1, high_y, pltpu.roll(v, rows_y - 1, 1)) - v
        dz = jnp.where(at_z == rows_z - 1, 0.0, pltpu.roll(v, rows_z - 1, 2)) - v
        return dx, dy, dz

    u = u_ref[...]
    halos_u = halo_wait(0, halo_u)
    grads_u = grads_of(u, halos_u)
    norm = sum(total(d * mask) ** 2 for d in grads_u)
    spread_start(0, jnp.where(lane == g, norm, 0.0))

    most = cells.at[pl.ds(0, planes * (n_sub - 1))]
    pltpu.make_async_copy(most, most, crecv).wait()
    pltpu.make_async_copy(most, most, csend).wait()
    for copy in fetches:
        copy.wait()
    packed = cells[...]
    turned = [packed] + [pltpu.roll(packed, i * side, 2) for i in range(1, 4)]
    set_of = lax.broadcasted_iota(jnp.int32, packed.shape, 2) // side

    def unpack(at):
        out = turned[(0 - at) % 4]
        for j in range(1, 4):
            out = jnp.where(set_of == j, turned[(j - at) % 4], out)
        return out

    def planes_of(low, high):
        parts = []
        for i in range(n_sub):
            parts += [unpack(low)[i * planes : (i + 1) * planes]]
            parts += [unpack(high)[i * planes : (i + 1) * planes]]
        return jnp.concatenate(parts, 0)

    cell_phase, cell_soften = planes_of(0, 2), planes_of(1, 3)
    norms = jnp.sum(spread_wait(0), axis=0)
    strength = jnp.sum(jnp.where(owner_ref[...] == g, norms, 0.0), axis=1, keepdims=True)
    cond = cell_phase / (1.0 + cell_soften * strength)
    shift_k = cond - K0
    cube = (side, side, 128)
    cell_lane = lax.broadcasted_iota(jnp.int32, cube, 2)
    group = cell_lane // side
    in_group = lax.rem(cell_lane, side)

    def ahead(v, axis):
        if axis == 0:
            return jnp.concatenate([v[1:], v[:1]], 0)
        if axis == 1:
            return pltpu.roll(v, side - 1, 1)
        return jnp.where(in_group == side - 1, pltpu.roll(v, side - 1, 2), pltpu.roll(v, 127, 2))

    def behind(v, axis):
        if axis == 0:
            return jnp.concatenate([v[-1:], v[:-1]], 0)
        if axis == 1:
            return pltpu.roll(v, 1, 1)
        return jnp.where(in_group == 0, pltpu.roll(v, 129 - side, 2), pltpu.roll(v, 1, 2))

    wide = side * 8
    tz = table_ref[4, 0:128, 0:128], table_ref[5, 0:128, 0:128]
    ty = table_ref[0], table_ref[1]
    tx = table_ref[2], table_ref[3]

    def right(v):
        high, low = split(v.reshape(side * side, 128))
        return (mm(high, tz[0]) + mm(low, tz[0]) + mm(high, tz[1])).reshape(cube)

    def left(t, v):
        high, low = split(v)
        return mm(t[0], high) + mm(t[0], low) + mm(t[1], high)

    def along_y(v):
        flat = v.reshape(side * side, 128)
        parts = [left(ty, flat[i : i + wide]) for i in range(0, side * side, wide)]
        return jnp.concatenate(parts, 0).reshape(cube)

    def along_x(v):
        parts = [
            left(tx, v[:, i : i + 8].reshape(wide, 128)).reshape(side, 8, 128)
            for i in range(0, side, 8)
        ]
        return jnp.concatenate(parts, 1)

    def solve(div):
        spectrum = along_x(along_y(right(div))) * inverse_ref[...]
        return right(along_y(along_x(spectrum)))

    def div_of(phi):
        out = 0.0
        for axis in range(3):
            tau = shift_k * (ahead(phi, axis) - phi)
            out = out + tau - behind(tau, axis)
        return out

    back = jnp.where(group == 0, behind(shift_k, 0), shift_k)
    back = jnp.where(group == 1, behind(shift_k, 1), back)
    back = jnp.where(group == 2, behind(shift_k, 2), back)
    div1 = shift_k - back
    phi1 = solve(div1)
    div2 = div_of(phi1)
    phi2 = solve(div2)
    div3 = div_of(phi2)
    first, second = div1 + div2, div2 + div3
    points = float(side**3)
    mean = total(cond) / (points * (128 // side))
    entry = {}
    for turn in range(3):
        a = phi1 if turn == 0 else pltpu.roll(phi1, turn * side, 2)
        b = phi2 if turn == 0 else pltpu.roll(phi2, turn * side, 2)
        sums = jnp.sum(jnp.sum(a * first + b * second, axis=0), axis=0, keepdims=True)
        for j in range(turn, 3):
            value = -jnp.sum(
                jnp.where(lane // side == j, sums, 0.0), axis=1, keepdims=True
            ) / points
            entry[j - turn, j] = entry[j, j - turn] = value + mean if turn == 0 else value
    row = jnp.zeros((1, 128), F32)
    for i in range(3):
        for j in range(3):
            row = row + jnp.where(lane == 3 * i + j, entry[i, j], 0.0)
    tan_ref[g] = row

    def tangent_send(k, carry):
        pltpu.make_async_remote_copy(
            src_ref=tan_ref.at[g], dst_ref=tan_ref.at[g], send_sem=tsend, recv_sem=trecv,
            device_id={"grp": lax.rem(g + k, n_grp), "sub": s}, device_id_type=MESH,
        ).start()
        return carry

    lax.fori_loop(1, n_grp, tangent_send, 0)
    most = tan_ref.at[pl.ds(0, n_grp - 1)]
    pltpu.make_async_copy(most, most, trecv).wait()
    pltpu.make_async_copy(most, most, tsend).wait()
    tangents = tan_ref[...]
    which = lax.broadcasted_iota(jnp.int32, (n_grp, 1, 128), 0)

    def tensor(p):
        who = jnp.sum(jnp.where(lane == p, owner_ref[...], 0).astype(F32), axis=1, keepdims=True)
        mine = jnp.sum(jnp.where(which.astype(F32) == who, tangents, 0.0), axis=0)
        return {
            (i, j): jnp.sum(jnp.where(lane == 3 * i + j, mine, 0.0), axis=1, keepdims=True)
            for i in range(3) for j in range(i, 3)
        }

    t_own, t_before = tensor(g), tensor(lax.max(g - 1, 0))
    k00, k11, k22 = (k_own + mask * (t_own[i, i] - k_own) for i in range(3))
    k01, k02, k12 = (mask * t_own[i] for i in ((0, 1), (0, 2), (1, 2)))
    x00 = k_x + mask_x * (t_before[0, 0] - k_x)
    x01, x02 = mask_x * t_before[0, 1], mask_x * t_before[0, 2]
    y11 = k_y + mask_y * (t_own[1, 1] - k_y)
    y01, y12 = mask_y * t_own[0, 1], mask_y * t_own[1, 2]

    def operate(v, halos, grads):
        low_x, _, low_y, _, corner_x, corner_y = halos
        dx, dy, dz = grads
        q0 = k00 * dx + k01 * dy + k02 * dz
        q1 = k01 * dx + k11 * dy + k12 * dz
        q2 = k02 * dx + k12 * dy + k22 * dz
        edge_y, edge_z = at_y[0] == rows_y - 1, at_z[0] == rows_z - 1
        below_x = (
            x00 * (v[0] - low_x)
            + x01 * (jnp.where(edge_y, corner_x, pltpu.roll(low_x, rows_y - 1, 0)) - low_x)
            + x02 * (jnp.where(edge_z, 0.0, pltpu.roll(low_x, rows_z - 1, 1)) - low_x)
        )
        below_y = (
            y11 * (v[:, 0:1] - low_y)
            + y01 * (jnp.concatenate([low_y[1:], corner_y[None]], 0) - low_y)
            + y12
            * (jnp.where(at_z[:, 0:1] == rows_z - 1, 0.0, pltpu.roll(low_y, rows_z - 1, 2)) - low_y)
        )
        out = jnp.concatenate([below_x[None], q0[:-1]], 0) - q0
        out = out + jnp.where(at_y == 0, below_y, pltpu.roll(q1, 1, 1)) - q1
        out = out + jnp.where(at_z == 0, 0.0, pltpu.roll(q2, 1, 2)) - q2
        return out + SHIFT * v

    def picks(grads):
        return [total(d * mask) for d in grads]

    def row_of(values):
        out = jnp.zeros((1, 128), F32)
        for i, value in enumerate(values):
            out = out + jnp.where(lane == i, value, 0.0)
        return out

    def apply(stage, v, meanwhile=None):
        field[stage - 1] = v
        copies = halo_start(stage, field.at[stage - 1])
        if meanwhile is not None:
            meanwhile()
        halos = halo_wait(stage, copies)
        grads = grads_of(v, halos)
        return operate(v, halos, grads), picks(grads)

    def choose():
        for q in range(flux_ref.shape[0]):
            chosen[q] = jnp.sum(jnp.where(which == owners[q], tangents, 0.0), axis=0)

    r = [load_ref[...] - operate(u, halos_u, grads_u)]
    v, slope0 = apply(1, r[0], choose)
    r.append(v)
    v, slope1 = apply(2, r[1])
    r.append(v)
    x = point_x = 0.0
    p = gp = None
    gamma = alpha = r3_before = g2_before = None

    def steps(r, p, scalars, depth):
        (first, one), (second, two) = scalars
        p = r if p is None else [a + first * b for a, b in zip(r, p)]
        move = one * p[0]
        r = [r[j] - one * p[j + 1] for j in range(depth)]
        middle = r[-1]
        p = [a + second * b for a, b in zip(r, p)]
        move = move + two * p[0]
        r = [r[j] - two * p[j + 1] for j in range(depth - 1)]
        return r, p, move, middle

    blocks = CG_ITERS // 2
    for step in range(blocks):
        last = step == blocks - 1

        def send(step=step, r=r, p=p, slopes=slope0 + slope1):
            dots = [total(r[0] * r[0]), total(r[0] * r[1]), total(r[1] * r[1]), total(r[1] * r[2])]
            if p is not None:
                dots += [total(r[1] * p[1]), total(p[1] * p[1])]
                dots += [total(p[1] * r[2]), total(p[1] * p[2])]
            else:
                dots += [jnp.zeros((1, 1), F32)] * 4
            spread_start(step + 1, row_of(dots + slopes))

        if last:
            send()
        else:
            r3, slope0 = apply(3 + 2 * step, r[2], send)
            r4, slope1 = apply(4 + 2 * step, r3)
        got = spread_wait(step + 1)
        sums = jnp.sum(got, axis=0)
        m00, m01, m11, m12, c11, d11, c12, d12 = (sums[:, i : i + 1] for i in range(8))
        if step == 0:
            first, one = jnp.zeros((1, 1), F32), m00 / m01
        else:
            first = m00 / gamma
            one = m00 / (m01 - first * m00 / alpha)
        image_square = m11 + first * (2.0 * c11 + first * d11)
        cross = m11 + first * c11
        image_energy = m12 + first * (2.0 * c12 + first * d12)
        m00_next = one * one * image_square - m00
        m01_next = m01 - 2.0 * one * cross + one * one * image_energy
        second = m00_next / m00
        two = m00_next / (m01_next - second * m00_next / one)
        scalars = (first, one), (second, two)

        fresh = [got, pltpu.roll(got, 125, 2)]
        if step == 0:
            gr = fresh
        else:
            if gp is not None:
                gp = gp + [(g2_before - fresh[0]) / alpha_before]
            gr, gp, move, g2_before = steps(gr + fresh, gp, scalars_before, 3)
            point_x = point_x + move
        if last:
            (first, one), (second, two) = scalars
            q0 = gr[0] + first * gp[0]
            q1 = gr[1] + first * gp[1]
            point_x = point_x + one * q0 + two * (gr[0] - one * q1 + second * q0)

        if last:
            r, p, move, _ = steps(r, p, scalars, 2)
        else:
            if p is not None:
                p = p + [(r3_before - r3) / alpha]
            r, p, move, r3_before = steps(r + [r3, r4], p, scalars, 4)
        x = x + move
        scalars_before, alpha_before = scalars, alpha
        gamma, alpha = m00_next, two
    step_ref[...] = x
    res_ref[...] = r[0]
    points = flux_ref.shape[0]
    slope = jnp.sum(point_x.reshape(points, n_sub, 1, 128), axis=1)
    spot = lax.broadcasted_iota(jnp.int32, slope.shape, 2)
    product = 0.0
    for j in range(3):
        part = jnp.sum(jnp.where(spot == 8 + j, slope, 0.0), axis=2, keepdims=True)
        product = product + jnp.where((lax.rem(spot, 3) == j) & (spot < 9), chosen[...], 0.0) * part
    out = jnp.zeros_like(slope)
    for i in range(3):
        part = jnp.sum(jnp.where(spot // 3 == i, product, 0.0), axis=2, keepdims=True)
        out = out + jnp.where(spot == i, part, 0.0)
    flux_ref[...] = out


def tables(side):
    index = np.arange(side)
    angle = 2.0 * np.pi * (np.outer(index, index) % side) / side
    hartley = (np.cos(angle) + np.sin(angle)) / np.sqrt(side)
    wide = side * 8
    kinds = np.zeros((3, wide, wide), np.float64)
    kinds[0] = np.kron(np.eye(8), hartley)
    kinds[1] = np.kron(hartley, np.eye(8))
    kinds[2, :128, :128] = np.kron(np.eye(128 // side), hartley)
    kinds = kinds.astype(np.float32)
    high = kinds.astype(jnp.bfloat16)
    low = (kinds - high.astype(np.float32)).astype(jnp.bfloat16)
    table = np.stack([high, low], 1).reshape(6, wide, wide)
    line = 4.0 * np.sin(np.pi * index / side) ** 2
    lam = line[:, None, None] + line[None, :, None] + line[None, None, :]
    lam[0, 0, 0] = 1.0
    inverse = 1.0 / (K0 * lam)
    inverse[0, 0, 0] = 0.0
    return table, np.tile(inverse.astype(np.float32), (1, 1, 128 // side))


def body(displacement, load, kl_coef, damaged, owner, phase, soften):
    n_grp, n_sub = lax.axis_size("grp"), lax.axis_size("sub")
    count = n_grp * n_sub
    rows_x, rows_y, rows_z = displacement.shape
    planes = phase.shape[1]
    side = math.isqrt(phase.shape[2])
    table, inverse = tables(side)
    half = planes // 2
    cubes = [a.reshape(planes, side, side) for a in (phase, soften)]
    packed = jnp.concatenate([a[i : i + half] for i in (0, half) for a in cubes], axis=2)
    points = owner.shape[0]
    owners = jnp.pad(owner, (0, 128 - points), constant_values=-1).reshape(1, 128)
    vmem = pl.BlockSpec(memory_space=pltpu.VMEM)
    smem = pl.BlockSpec(memory_space=pltpu.SMEM)
    step_field, residual, rows, flux = pl.pallas_call(
        functools.partial(kernel, n_grp, n_sub, side),
        out_shape=[
            jax.ShapeDtypeStruct(displacement.shape, F32),
            jax.ShapeDtypeStruct(displacement.shape, F32),
            jax.ShapeDtypeStruct((n_grp, 1, 128), F32),
            jax.ShapeDtypeStruct((points, 1, 128), F32),
        ],
        in_specs=[smem] * 3 + [vmem] * 4 + [pl.BlockSpec(memory_space=pl.ANY)] * 2,
        out_specs=[vmem] * 4,
        scratch_shapes=[
            pltpu.VMEM((CG_ITERS, rows_x, rows_y, rows_z), F32),
            pltpu.VMEM((STAGES, 2, rows_x, 1, rows_z), F32),
            pltpu.VMEM((STAGES, 2, rows_y, rows_z), F32),
            pltpu.VMEM((STAGES, 2, rows_x, 1, rows_z), F32),
            pltpu.VMEM((STAGES, 2, 1, rows_z), F32),
            pltpu.VMEM((half * n_sub, side, 128), F32),
            pltpu.VMEM((CG_ITERS // 2 + 1, count, 1, 128), F32),
            pltpu.VMEM((points, 1, 128), F32),
            pltpu.VMEM(table.shape, BF16),
            pltpu.VMEM(inverse.shape, F32),
            pltpu.SemaphoreType.DMA((STAGES, 6)),
            pltpu.SemaphoreType.DMA((STAGES, 6)),
            pltpu.SemaphoreType.DMA,
            pltpu.SemaphoreType.DMA,
            pltpu.SemaphoreType.DMA((STAGES,)),
            pltpu.SemaphoreType.DMA((STAGES,)),
            pltpu.SemaphoreType.DMA,
            pltpu.SemaphoreType.DMA,
            pltpu.SemaphoreType.DMA((2,)),
        ],
        compiler_params=pltpu.CompilerParams(collective_id=0, has_side_effects=True),
    )(kl_coef, damaged, owner, displacement, load, owners, packed, jnp.asarray(table), jnp.asarray(inverse))
    return step_field, residual, rows[:, 0, :9], flux[:, 0, :3]


def solution(mesh):
    return jax.shard_map(
        body,
        mesh=mesh,
        in_specs=(
            P("grp", "sub", None), P("grp", "sub", None), P(), P(), P(),
            P("grp", "sub", None), P("grp", "sub", None),
        ),
        out_specs=(P("grp", "sub", None), P("grp", "sub", None), P(), P()),
        check_vma=False,
    )
```
